32 devices in a mesh: section: 4 (over z), dp: 4 (over x, core), tensor: 2 (over y).
Axes of the slice: x: 2, y: 2, z: 4, core: 2. Of those that a mesh axis runs over, the one named last changes fastest.
Arguments:
- activations: bfloat16 [4, 512, 4096], P('section', 'dp', 'tensor'), may hold values from -32 to 32
- norm_gain: float32 [4, 4096], P('section', 'tensor'), may hold values from 0.5 to 2
- weights: bfloat16 [4, 4096, 1024], P('section', 'tensor'), may hold values from -0.09375 to 0.09375
- cotangent: bfloat16 [4, 512, 1024], P('section', 'dp'), may hold values from -16 to 16
- top_grad: bfloat16 [512, 4096], P('dp', 'tensor'), may hold values from -6 to 6
- owner_slot: int32 [4, 2, 13], P('section', 'tensor'), may hold values from 0 to 15, as said below
- sweeps: int32 [4, 2, 4], P('section', 'tensor'), may hold values from 3 to 6
Outputs:
- input_grad: bfloat16 [4, 512, 4096], P('section', 'dp', 'tensor')
- preconditioned: bfloat16 [4, 4096, 1024], P('section', 'tensor')
The draws below stay inside these ranges and needn't reach their ends.
Inputs may be any that keep to these rules, and one draw needn't show every extreme that they name: For each section and tensor index the 13 entries are distinct; the unit is owned by data replica owner_slot // 4, so a replica owns at most 4 units, and some replica owns exactly 4.
All inputs are finite; a program needn't handle non-finite values.
Results may differ from the reference program's by a relative error of at most 0.035.
Values may be sent and summed in bfloat16 or wider, within the bound.
No kernel may reach another device: no remote copies, remote signals or barrier semaphores. Data moves between devices by JAX's collectives and lax.ppermute only.
A program may use at most 128 MiB of HBM per device.

```python
import math
import jax
import jax.numpy as jnp
from jax import lax

D = 4096
KV = 1024
BLOCK = 512
ITERS = 6
TOK_DEV = 128
SECTIONS = 4
TOKENS = 512
NA = 4
NG = 2
UNITS = 13
CAP = 4
SLOTS = 16
N_DP = 4
N_TENSOR = 2


def draw_activations(key, part):
    key_base = jax.random.fold_in(key, 11)
    key_scale = jax.random.fold_in(key, 12)
    feature_ramp = 1.0 + 2.0 * jnp.arange(D, dtype=jnp.float32) / (D - 1)
    jitter = jnp.exp(jax.random.uniform(key_scale, (SECTIONS, 1, D), minval=-0.3, maxval=0.3))
    values_base = jax.random.normal(key_base, (SECTIONS, TOKENS, D), dtype=jnp.float32)
    return jnp.clip(values_base * feature_ramp * jitter, -32.0, 32.0).astype(jnp.bfloat16)


def draw_cotangent(key, part):
    key_base = jax.random.fold_in(key, 21)
    key_scale = jax.random.fold_in(key, 22)
    column_scale = jnp.exp(jax.random.uniform(key_scale, (SECTIONS, 1, KV), minval=-0.7, maxval=0.7))
    values_base = jax.random.normal(key_base, (SECTIONS, TOKENS, KV), dtype=jnp.float32)
    return jnp.clip(values_base * column_scale, -16.0, 16.0).astype(jnp.bfloat16)


def draw_owner_slot(key, part):
    key_list = jax.random.split(jax.random.fold_in(key, 31), SECTIONS * N_TENSOR)

    def one_table(single_key):
        return jax.random.permutation(single_key, SLOTS)[:UNITS]
    tables = jax.vmap(one_table)(key_list)
    return tables.reshape(SECTIONS, N_TENSOR, UNITS).astype(jnp.int32)


def set_ends(drawn, key, smallest, high):
    index_at = [jax.random.randint(jax.random.fold_in(key, axis), (), 0, length) for axis, length in enumerate(drawn.shape)]
    widest = drawn.shape.index(max(drawn.shape))
    next_to = index_at[:widest] + [(index_at[widest] + 1) % drawn.shape[widest]] + index_at[widest + 1:]
    return drawn.at[tuple(index_at)].set(smallest).at[tuple(next_to)].set(high)


def level_of(key, shape, cuts, least, top_value):
    def one(position, shards_of):
        draws = jax.random.uniform(jax.random.fold_in(jax.random.fold_in(key, 6), position), (shards_of,), jnp.float32, least / len(cuts), top_value / len(cuts))
        return jnp.repeat(jnp.exp(draws), shape[position] // shards_of).reshape((-1,) + (1,) * (len(shape) - position - 1))

    gain = one(*cuts[0])
    for cut in cuts[1:]:
        gain = gain * one(*cut)
    return gain


def noise(rng, extent, scale, limit, shards=(), kind=jnp.bfloat16):
    values = jax.random.normal(rng, extent, jnp.float32) * scale
    if len(shards) > 0:
        values = level_of(rng, extent, shards, -0.22, 0.18) * values
    return jnp.clip(values, min=-limit, max=limit).astype(kind)


def setup_inputs(seed: int = 0) -> dict:
    seeds = jax.random.split(jax.random.key(seed), 8)
    activations = draw_activations(jax.random.fold_in(seeds[7], 71), 0)
    norm_gain = jnp.clip(jnp.exp(math.log(2.0) - 1.3862944 * jax.random.uniform(seeds[1], (SECTIONS, D), jnp.float32) ** level_of(seeds[1], (SECTIONS, D), ((0, 4), (1, 2)), -0.2, 0.2)), 0.5, 2.0)
    weights = noise(seeds[2], (SECTIONS, D, KV), D ** -0.5, 0.09375, ((0, 4), (1, 2)))
    cotangent = draw_cotangent(jax.random.fold_in(seeds[7], 71), 0)
    top_grad = noise(seeds[4], (TOKENS, D), 1.0, 6.0, ((0, 4), (1, 2)))
    owner_slot = draw_owner_slot(jax.random.fold_in(seeds[7], 71), 0)
    sweeps = set_ends(jax.random.randint(seeds[6], (SECTIONS, N_TENSOR, N_DP), ITERS - 3, ITERS + 1), jax.random.fold_in(seeds[6], 1), ITERS - 3, ITERS).astype(jnp.int32)
    return {"activations": activations, "norm_gain": norm_gain, "weights": weights, "cotangent": cotangent, "top_grad": top_grad, "owner_slot": owner_slot, "sweeps": sweeps}


EPSILON = 1e-05
DAMPING = 0.05
HIGHEST_PREC = lax.Precision.HIGHEST

def rounded(values):
    return lax.optimization_barrier(values.astype(jnp.bfloat16)).astype(jnp.float32)

def newton_schulz(matrices, limits):
    order_size = matrices.shape[-1]
    identity = jnp.eye(order_size, dtype=jnp.float32)
    frobenius = jnp.sqrt(lax.optimization_barrier(jnp.sum(matrices * matrices, axis=(1, 2))))
    approx = identity[None] / frobenius[:, None, None]
    for each_sweep in range(ITERS):
        product = jnp.einsum('cij,cjk->cik', matrices, approx, precision=HIGHEST_PREC)
        update = jnp.einsum('cij,cjk->cik', approx, 2.0 * identity[None] - product, precision=HIGHEST_PREC)
        approx = jnp.where((each_sweep < limits)[:, None, None], update, approx)
    return approx

def reference(activations, norm_gain, weights, cotangent, top_grad, owner_slot, sweeps):
    identity = jnp.eye(BLOCK, dtype=jnp.float32)
    terms_all = []
    pre_blocks = []
    for section_index in range(SECTIONS):
        inputs = activations[section_index].astype(jnp.float32)
        gain_row = norm_gain[section_index]
        squares = lax.optimization_barrier(jnp.sum(inputs * inputs, axis=1))
        inverse_rms = lax.rsqrt(squares / D + EPSILON)
        normed = (inputs * inverse_rms[:, None] * gain_row[None]).astype(jnp.bfloat16)
        upstream_v = cotangent[section_index]
        upstream = lax.dot_general(upstream_v, weights[section_index], (((1,), (1,)), ((), ())), preferred_element_type=jnp.float32)
        scaled = upstream * gain_row[None]
        inner_sum = lax.optimization_barrier(jnp.sum(scaled * inputs, axis=1))
        terms_all.append(inverse_rms[:, None] * scaled - inputs * (inverse_rms ** 3 * inner_sum / D)[:, None])
        normed_parts = normed.reshape(N_DP, TOK_DEV, D // BLOCK, BLOCK).astype(jnp.float32)
        value_parts = upstream_v.reshape(N_DP, TOK_DEV, NG, BLOCK).astype(jnp.float32)
        feature_sum = lax.optimization_barrier(jnp.sum(rounded(jnp.einsum('rtia,rtib->riab', normed_parts, normed_parts)), axis=0))
        value_sum = lax.optimization_barrier(jnp.sum(rounded(jnp.einsum('rtja,rtjb->rjab', value_parts, value_parts)), axis=0))
        grad_sum = lax.optimization_barrier(jnp.sum(rounded(jnp.einsum('rtia,rtjb->rijab', normed_parts, value_parts)), axis=0))
        feature_limits = []
        value_limits = []
        for half_index in range(N_TENSOR):
            counts = sweeps[section_index, half_index]
            owners = (owner_slot[section_index, half_index, :NA + 1] // CAP).astype(jnp.int32)
            unit_limits = jnp.take(counts, owners)
            feature_limits.append(unit_limits[:NA])
            value_limits.append(unit_limits[NA:NA + 1])
        feature_inv = newton_schulz(feature_sum / TOKENS + DAMPING * identity[None], jnp.concatenate(feature_limits)).astype(jnp.bfloat16)
        value_inv = newton_schulz(value_sum / TOKENS + DAMPING * identity[None], jnp.concatenate(value_limits)).astype(jnp.bfloat16)
        grad_round = grad_sum.astype(jnp.bfloat16)
        left_part = jnp.einsum('iab,ijbc->ijac', feature_inv.astype(jnp.float32), grad_round.astype(jnp.float32)).astype(jnp.bfloat16)
        result = jnp.einsum('ijac,jcd->iajd', left_part.astype(jnp.float32), value_inv.astype(jnp.float32)).astype(jnp.bfloat16)
        pre_blocks.append(result.reshape(D, KV))
    terms_stack = jnp.stack(terms_all)
    inclusive = jnp.flip(jnp.cumsum(jnp.flip(terms_stack, 0), axis=0), 0)
    input_grad = (top_grad.astype(jnp.float32)[None] + inclusive).astype(jnp.bfloat16)
    return (input_grad, jnp.stack(pre_blocks))
```

```python
import functools

import jax
import jax.numpy as jnp
from jax import lax
from jax.experimental import pallas as pl
from jax.experimental.pallas import tpu as pltpu
from jax.sharding import PartitionSpec as P

BLOCK = 512
EPSILON = 1e-05
DAMPING = 0.05
RELAY_CHUNKS = 2
GATHER_CHUNKS = 2


def doubled(pieces, axis):
    count = lax.axis_size(axis)
    step = count // 2
    while step >= 1:
        pairs = [(k, k ^ step) for k in range(count)]
        pieces = pieces + [lax.ppermute(piece, axis, pairs) for piece in pieces]
        step //= 2
    return pieces


def other_half(value, axis):
    return lax.ppermute(value, axis, [(0, 1), (1, 0)])


def relay(own_term, axis):
    count = lax.axis_size(axis)
    total = None
    running = own_term
    for source in range(count - 1, 0, -1):
        arrived = lax.ppermute(running.astype(jnp.bfloat16), axis, [(source, source - 1)])
        arrived = arrived.astype(jnp.float32)
        total = arrived if total is None else total + arrived
        running = own_term + total
    return running


def first_dim_product(left, right):
    return lax.dot_general(
        left, right, (((0,), (0,)), ((), ())), preferred_element_type=jnp.float32
    )


def product(left, right):
    return jnp.dot(left, right, preferred_element_type=jnp.float32)


def inverse_of(tokens, limit, state, halves):
    count, order = tokens.shape
    rows = lax.broadcasted_iota(jnp.int32, (order, order), 0)
    columns = lax.broadcasted_iota(jnp.int32, (order, order), 1)
    diagonal = rows == columns
    matrix = first_dim_product(tokens, tokens) * (1.0 / count)
    matrix = matrix + jnp.where(diagonal, DAMPING, 0.0)
    scale = lax.rsqrt(jnp.sum(matrix * matrix))
    first = matrix * scale
    start = jnp.where(diagonal, 2.0, 0.0) - first
    first_half = first.astype(jnp.bfloat16)
    state[0] = start
    halves[0:order] = start.astype(jnp.bfloat16)
    grown = 2.0 * first - product(first_half, first_half)
    state[1] = grown
    halves[order:] = grown.astype(jnp.bfloat16)

    def sweep(k, carry):
        change = product(halves[...], halves[order:])
        approx = 2.0 * state[0] - change[:order]
        grown = 2.0 * state[1] - change[order:]
        state[0] = approx
        state[1] = grown
        halves[0:order] = approx.astype(jnp.bfloat16)
        halves[order:] = grown.astype(jnp.bfloat16)
        return carry

    lax.fori_loop(2, limit, sweep, 0)
    last = 2.0 * state[0] - product(halves[0:order], halves[order:])
    return (last * scale).astype(jnp.bfloat16)


def value_kernel(limits, *refs, pieces):
    tokens = jnp.concatenate([ref[...] for ref in refs[:pieces]], axis=0)
    out, state, halves = refs[pieces:]
    out[0] = inverse_of(tokens, limits[pl.program_id(0)], state, halves)


def feature_kernel(table, counts, *refs, pieces, first, capacity):
    normed = jnp.concatenate([ref[...] for ref in refs[:pieces]], axis=0)
    values = refs[pieces : 2 * pieces]
    value_inverse = refs[2 * pieces]
    out, state, halves = refs[-3:]
    owner = table[pl.program_id(0) + first] // capacity
    inverse = inverse_of(normed, counts[owner], state, halves)
    cotangent = jnp.concatenate([ref[...] for ref in values], axis=0)
    grad = first_dim_product(normed, cotangent).astype(jnp.bfloat16)
    left = product(inverse, grad).astype(jnp.bfloat16)
    for j in range(value_inverse.shape[0]):
        span = slice(j * BLOCK, (j + 1) * BLOCK)
        out[:, span] = product(left[:, span], value_inverse[j]).astype(jnp.bfloat16)


def scratch():
    return [
        pltpu.VMEM((2, BLOCK, BLOCK), jnp.float32),
        pltpu.VMEM((2 * BLOCK, BLOCK), jnp.bfloat16),
    ]


def invert_values(limits, pieces):
    tokens, width = pieces[0].shape
    blocks = width // BLOCK
    return pl.pallas_call(
        functools.partial(value_kernel, pieces=len(pieces)),
        grid_spec=pltpu.PrefetchScalarGridSpec(
            num_scalar_prefetch=1,
            grid=(blocks,),
            in_specs=[pl.BlockSpec((tokens, BLOCK), lambda i, *_: (0, i))] * len(pieces),
            out_specs=pl.BlockSpec((1, BLOCK, BLOCK), lambda i, *_: (i, 0, 0)),
            scratch_shapes=scratch(),
        ),
        out_shape=jax.ShapeDtypeStruct((blocks, BLOCK, BLOCK), jnp.bfloat16),
        cost_estimate=pl.CostEstimate(
            flops=22 * blocks * BLOCK**3, bytes_accessed=4 * blocks * BLOCK**2, transcendentals=0
        ),
        name="value_inverses",
    )(limits, *pieces)


def precondition(table, counts, normed, cotangents, value_inverses, first, rows, capacity, before):
    tokens, width = normed[0].shape
    blocks = width // BLOCK
    value_width = cotangents[0].shape[1]
    pieces = len(normed)
    args = [table, counts, *normed, *cotangents, value_inverses]
    in_specs = [pl.BlockSpec((tokens, BLOCK), lambda i, *_: (0, i))] * pieces
    in_specs += [pl.BlockSpec((tokens, value_width), lambda i, *_: (0, 0))] * pieces
    in_specs += [pl.BlockSpec(value_inverses.shape, lambda i, *_: (0, 0, 0))]
    aliases = {}
    if before is not None:
        aliases = {len(args): 0}
        args.append(before)
        in_specs.append(pl.BlockSpec(memory_space=pl.ANY))
    return pl.pallas_call(
        functools.partial(feature_kernel, pieces=pieces, first=first, capacity=capacity),
        grid_spec=pltpu.PrefetchScalarGridSpec(
            num_scalar_prefetch=2,
            grid=(blocks,),
            in_specs=in_specs,
            out_specs=pl.BlockSpec((BLOCK, value_width), lambda i, *_: (i + first, 0)),
            scratch_shapes=scratch(),
        ),
        out_shape=jax.ShapeDtypeStruct((rows, value_width), jnp.bfloat16),
        input_output_aliases=aliases,
        cost_estimate=pl.CostEstimate(
            flops=34 * blocks * BLOCK**3, bytes_accessed=8 * blocks * BLOCK**2, transcendentals=0
        ),
        name="precondition",
    )(*args)


def on_device(activations, norm_gain, weights, cotangent, top_grad, owner_slot, sweeps):
    inputs = activations[0].astype(jnp.float32)
    gain_row = norm_gain[0]
    weight_half = weights[0]
    upstream_v = cotangent[0]
    slot_table = owner_slot[0, 0]
    replica_limits = sweeps[0, 0]
    token_count, half_width = inputs.shape
    value_width = weight_half.shape[1]
    tensor_size = lax.axis_size("tensor")
    replica_count = lax.axis_size("dp")
    full_width = half_width * tensor_size
    feature_blocks = half_width // BLOCK
    value_blocks = value_width // BLOCK
    unit_count = feature_blocks + 1 + feature_blocks * value_blocks
    capacity = (unit_count + replica_count - 1) // replica_count

    cotangents = doubled([upstream_v], "dp")

    value_owner = slot_table[feature_blocks] // capacity
    replica_ids = jnp.arange(replica_count, dtype=jnp.int32)
    value_limit = jnp.sum(jnp.where(replica_ids == value_owner, replica_limits, 0))
    own_squares = jnp.sum(inputs * inputs, axis=1)
    own_row = jnp.stack(
        [own_squares, jnp.broadcast_to(value_limit.astype(jnp.float32), own_squares.shape)]
    )
    other_row = other_half(own_row, "tensor")
    squares = own_squares + other_row[0]
    other_limit = other_row[1, 0].astype(jnp.int32)
    tensor_rank = lax.axis_index("tensor")
    value_limits = jnp.where(
        jnp.arange(value_blocks, dtype=jnp.int32) == tensor_rank, value_limit, other_limit
    )
    inverse_rms = lax.rsqrt(squares / full_width + EPSILON)

    normed = (inputs * inverse_rms[:, None] * gain_row[None]).astype(jnp.bfloat16)
    part = half_width // GATHER_CHUNKS
    normed_parts = [
        doubled([normed[:, k * part : (k + 1) * part]], "dp") for k in range(GATHER_CHUNKS)
    ]

    upstream = lax.dot_general(
        upstream_v, weight_half, (((1,), (1,)), ((), ())), preferred_element_type=jnp.float32
    )
    scaled = upstream * gain_row[None]
    own_inner = jnp.sum(scaled * inputs, axis=1)
    inner_sum = own_inner + other_half(own_inner[None], "tensor")[0]
    coefficient = inverse_rms * inverse_rms * inverse_rms * inner_sum / full_width
    own_term = inverse_rms[:, None] * scaled - inputs * coefficient[:, None]
    piece = half_width // RELAY_CHUNKS
    sums = [
        relay(own_term[:, k * piece : (k + 1) * piece], "section") for k in range(RELAY_CHUNKS)
    ]
    input_grad = (top_grad.astype(jnp.float32) + jnp.concatenate(sums, axis=1)).astype(jnp.bfloat16)

    value_inverses = invert_values(value_limits, cotangents)
    output = None
    for k in range(GATHER_CHUNKS):
        output = precondition(
            slot_table,
            replica_limits,
            normed_parts[k],
            cotangents,
            value_inverses,
            k * (part // BLOCK),
            half_width,
            capacity,
            output,
        )
    return (input_grad[None], output[None])


def solution(mesh):
    placed = (
        P("section", "dp", "tensor"),
        P("section", "tensor"),
        P("section", "tensor", None),
        P("section", "dp", None),
        P("dp", "tensor"),
        P("section", "tensor", None),
        P("section", "tensor", None),
    )
    return jax.shard_map(
        on_device,
        mesh=mesh,
        in_specs=placed,
        out_specs=(P("section", "dp", "tensor"), P("section", "tensor", None)),
        check_vma=False,
    )
```

```python
import functools

import jax
import jax.numpy as jnp
from jax import lax
from jax.experimental import pallas as pl
from jax.experimental.pallas import tpu as pltpu
from jax.sharding import PartitionSpec as P


BLOCK = 512
EPSILON = 1e-05
DAMPING = 0.05
LANES = 128
STAT_ROWS = 8
RELAY_CHUNKS = 2
RELAY_LAG = 1
VMEM_LIMIT = 24 * 2**20


def flipped(value, axis, bit):
    count = lax.axis_size(axis)
    return lax.ppermute(value, axis, [(k, k ^ bit) for k in range(count)])


def higher_bits(axis):
    bit = 2
    while bit < lax.axis_size(axis):
        yield bit
        bit *= 2


def first_dim_product(left, right):
    return lax.dot_general(
        left, right, (((0,), (0,)), ((), ())), preferred_element_type=jnp.float32
    )


def product(left, right):
    return jnp.dot(left, right, preferred_element_type=jnp.float32)


def inverse_of(tokens, limit, state, halves):
    count, order = tokens.shape
    rows = lax.broadcasted_iota(jnp.int32, (order, order), 0)
    columns = lax.broadcasted_iota(jnp.int32, (order, order), 1)
    diagonal = rows == columns
    matrix = first_dim_product(tokens, tokens) * (1.0 / count)
    matrix = matrix + jnp.where(diagonal, DAMPING, 0.0)
    scale = lax.rsqrt(jnp.sum(matrix * matrix))
    first = matrix * scale
    start = jnp.where(diagonal, 2.0, 0.0) - first
    first_half = first.astype(jnp.bfloat16)
    state[0] = start
    halves[0:order] = start.astype(jnp.bfloat16)
    grown = 2.0 * first - product(first_half, first_half)
    state[1] = grown
    halves[order:] = grown.astype(jnp.bfloat16)

    def sweep(k, carry):
        change = product(halves[...], halves[order:])
        approx = 2.0 * state[0] - change[:order]
        grown = 2.0 * state[1] - change[order:]
        state[0] = approx
        state[1] = grown
        halves[0:order] = approx.astype(jnp.bfloat16)
        halves[order:] = grown.astype(jnp.bfloat16)
        return carry

    lax.fori_loop(2, limit, sweep, 0)
    last = 2.0 * state[0] - product(halves[0:order], halves[order:])
    return (last * scale).astype(jnp.bfloat16)


def upstream_kernel(
    table, counts, cot_hbm, weight_hbm, act_hbm, gain_hbm, scaled_ref, stats_ref, cot, weight, act, gain, sems, *, position, capacity
):
    tokens, width = act.shape
    blocks = width // BLOCK
    small = [
        pltpu.make_async_copy(source, target, sems.at[k])
        for k, (source, target) in enumerate(((act_hbm, act), (cot_hbm, cot), (gain_hbm, gain)))
    ]
    large = [
        pltpu.make_async_copy(
            weight_hbm.at[pl.ds(k * BLOCK, BLOCK)],
            weight.at[pl.ds(k * BLOCK, BLOCK)],
            sems.at[3 + k],
        )
        for k in range(blocks)
    ]
    for copy in small + large:
        copy.start()
    small[0].wait()
    squares = jnp.zeros((tokens, LANES), jnp.float32)
    for k in range(width // LANES):
        inputs = act[:, k * LANES : (k + 1) * LANES].astype(jnp.float32)
        squares += inputs * inputs
    limit = counts[table[position] // capacity].astype(jnp.float32)
    stats_ref[...] = jnp.full(stats_ref.shape, limit, jnp.float32)
    stats_ref[0:1] = jnp.sum(squares.T, axis=0, keepdims=True)
    small[1].wait()
    small[2].wait()
    inner = jnp.zeros((tokens, LANES), jnp.float32)
    for k in range(blocks):
        span = slice(k * BLOCK, (k + 1) * BLOCK)
        large[k].wait()
        upstream = lax.dot_general(
            cot[...], weight[span], (((1,), (1,)), ((), ())), preferred_element_type=jnp.float32
        )
        scaled = upstream * gain[:, span]
        scaled_ref[:, span] = scaled
        for j in range(BLOCK // LANES):
            lanes = slice(j * LANES, (j + 1) * LANES)
            start = k * BLOCK + j * LANES
            inner += scaled[:, lanes] * act[:, start : start + LANES].astype(jnp.float32)
    stats_ref[1:2] = jnp.sum(inner.T, axis=0, keepdims=True)


SMEM = pl.BlockSpec(memory_space=pltpu.SMEM)
VMEM = pl.BlockSpec(memory_space=pltpu.VMEM)
HBM = pl.BlockSpec(memory_space=pltpu.HBM)


def in_hbm(*arrays):
    return [pltpu.with_memory_space_constraint(array, pltpu.HBM) for array in arrays]


def in_vmem(*arrays):
    return [pltpu.with_memory_space_constraint(array, pltpu.VMEM) for array in arrays]


def upstream_of(table, counts, cotangent, weights, activations, gain, position, capacity):
    tokens, value_width = cotangent.shape
    width = weights.shape[0]
    return pl.pallas_call(
        functools.partial(upstream_kernel, position=position, capacity=capacity),
        in_specs=[SMEM, SMEM, HBM, HBM, HBM, HBM],
        out_specs=[VMEM, VMEM],
        out_shape=[
            jax.ShapeDtypeStruct((tokens, width), jnp.float32),
            jax.ShapeDtypeStruct((STAT_ROWS, tokens), jnp.float32),
        ],
        scratch_shapes=[
            pltpu.VMEM(cotangent.shape, cotangent.dtype),
            pltpu.VMEM(weights.shape, weights.dtype),
            pltpu.VMEM(activations.shape, activations.dtype),
            pltpu.VMEM(gain.shape, gain.dtype),
            pltpu.SemaphoreType.DMA((3 + width // BLOCK,)),
        ],
        compiler_params=pltpu.CompilerParams(vmem_limit_bytes=VMEM_LIMIT),
        cost_estimate=pl.CostEstimate(
            flops=2 * tokens * width * value_width,
            bytes_accessed=2 * width * value_width + 8 * tokens * width,
            transcendentals=0,
        ),
        name="upstream",
    )(*in_hbm(table, counts, cotangent, weights, activations, gain))


def column(row):
    return jnp.broadcast_to(row, (LANES, row.shape[1])).T[:, :1]


def terms_kernel(core, scaled_ref, act_ref, gain_ref, own_ref, other_ref, term_ref, *refs, full_width):
    normed, first_sent, pieces = refs[-1], refs[-2], refs[:-2]
    squares = own_ref[0:1] + other_ref[0:1]
    inner_sum = own_ref[1:2] + other_ref[1:2]
    inverse_rms = lax.rsqrt(squares * (1.0 / full_width) + EPSILON)
    coefficient = inverse_rms * inverse_rms * inverse_rms * inner_sum * (1.0 / full_width)
    inverse_rms, coefficient = column(inverse_rms), column(coefficient)
    inputs = act_ref[...].astype(jnp.float32)
    normed[...] = (inputs * inverse_rms * gain_ref[...]).astype(jnp.bfloat16)
    term = inverse_rms * scaled_ref[...] - inputs * coefficient
    term_ref[...] = term.astype(jnp.bfloat16)
    first_sent[...] = term[: first_sent.shape[0]].astype(jnp.bfloat16)
    half = normed.shape[1] // 2
    blocks = half // BLOCK
    for k in range(blocks):
        mine = pl.multiple_of(core[0] * half + k * BLOCK, BLOCK)
        theirs = pl.multiple_of((1 - core[0]) * half + k * BLOCK, BLOCK)
        pieces[k][...] = normed[:, pl.ds(mine, BLOCK)]
        pieces[blocks + k][...] = normed[:, pl.ds(theirs, BLOCK)]


def terms_of(core, scaled, activations, gain, own_stats, other_stats, full_width):
    tokens, width = scaled.shape
    blocks = width // BLOCK
    smem = pl.BlockSpec(memory_space=pltpu.SMEM)
    vmem = pl.BlockSpec(memory_space=pltpu.VMEM)
    outs = pl.pallas_call(
        functools.partial(terms_kernel, full_width=full_width),
        in_specs=[smem] + [vmem] * 5,
        out_specs=[vmem] * (2 + blocks),
        out_shape=[jax.ShapeDtypeStruct((tokens, width), jnp.bfloat16)]
        + [jax.ShapeDtypeStruct((tokens, BLOCK), jnp.bfloat16)] * blocks
        + [jax.ShapeDtypeStruct((tokens // RELAY_CHUNKS, width), jnp.bfloat16)],
        scratch_shapes=[pltpu.VMEM((tokens, width), jnp.bfloat16)],
        compiler_params=pltpu.CompilerParams(vmem_limit_bytes=VMEM_LIMIT),
        cost_estimate=pl.CostEstimate(
            flops=8 * tokens * width, bytes_accessed=10 * tokens * width, transcendentals=0
        ),
        name="terms",
    )(core, *in_vmem(scaled, activations, gain, own_stats, other_stats))
    return outs[0], outs[-1], outs[1 : 1 + blocks // 2], outs[1 + blocks // 2 : -1]


def relay(term, first_sent, axis):
    count, index = lax.axis_size(axis), lax.axis_index(axis)
    rows = term.shape[0] // RELAY_CHUNKS
    arrived = []
    for wave in range(RELAY_CHUNKS + RELAY_LAG * (count - 2)):
        chunk = jnp.clip(wave - RELAY_LAG * (count - 1 - index), 0, RELAY_CHUNKS - 1)
        sent = lax.dynamic_slice_in_dim(term, chunk * rows, rows, 0) if wave else first_sent
        if wave >= RELAY_LAG:
            before = arrived[wave - RELAY_LAG].astype(jnp.float32)
            sent = (sent.astype(jnp.float32) + before).astype(jnp.bfloat16)
        pairs = [(k, k - 1) for k in range(1, count)]
        arrived.append(lax.ppermute(sent, axis, pairs))
    return arrived


def finish_kernel(section, top_ref, term_ref, *refs, sections):
    arrived, out = refs[:-1], refs[-1]
    rows = arrived[0].shape[0]
    for chunk in range(RELAY_CHUNKS):
        span = slice(chunk * rows, (chunk + 1) * rows)
        own = top_ref[span].astype(jnp.float32) + term_ref[span].astype(jnp.float32)

        @pl.when(section[0] == sections - 1)
        def _(span=span, own=own):
            out[span] = own.astype(jnp.bfloat16)

        for place in range(sections - 1):
            later = arrived[chunk + RELAY_LAG * (sections - 2 - place)]

            @pl.when(section[0] == place)
            def _(span=span, own=own, later=later):
                out[span] = (own + later[...].astype(jnp.float32)).astype(jnp.bfloat16)


def finish(section, sections, top_grad, term, arrived):
    vmem = pl.BlockSpec(memory_space=pltpu.VMEM)
    return pl.pallas_call(
        functools.partial(finish_kernel, sections=sections),
        in_specs=[pl.BlockSpec(memory_space=pltpu.SMEM)] + [vmem] * (2 + len(arrived)),
        out_specs=vmem,
        out_shape=jax.ShapeDtypeStruct(term.shape, jnp.bfloat16),
        compiler_params=pltpu.CompilerParams(vmem_limit_bytes=VMEM_LIMIT),
        cost_estimate=pl.CostEstimate(
            flops=2 * term.size, bytes_accessed=8 * term.size, transcendentals=0
        ),
        name="finish",
    )(section, *in_vmem(top_grad, term, *arrived))


def scratch():
    return [
        pltpu.VMEM((2, BLOCK, BLOCK), jnp.float32),
        pltpu.VMEM((2 * BLOCK, BLOCK), jnp.bfloat16),
    ]


def row_copies(pieces, target, sems, first=0):
    rows = target.shape[0] // len(pieces)
    return [
        pltpu.make_async_copy(piece, target.at[pl.ds(k * rows, rows)], sems.at[first + k])
        for k, piece in enumerate(pieces)
    ]


def value_kernel(place, own_stats, other_stats, *refs, pieces):
    span = pl.ds(pl.multiple_of(place[0] * BLOCK, BLOCK), BLOCK)
    out, state, halves, tokens, sems = refs[pieces:]
    copies = row_copies([ref.at[:, span] for ref in refs[:pieces]], tokens, sems)
    for copy in copies:
        copy.start()
    for copy in copies:
        copy.wait()
    own_limit, other_limit = jnp.max(own_stats[2:3]), jnp.max(other_stats[2:3])
    limit = jnp.where(place[0] == place[1], own_limit, other_limit).astype(jnp.int32)
    out[...] = inverse_of(tokens[...], limit, state, halves)


def invert_value(place, own_stats, other_stats, pieces):
    return pl.pallas_call(
        functools.partial(value_kernel, pieces=len(pieces)),
        in_specs=[SMEM, VMEM, VMEM] + [HBM] * len(pieces),
        out_specs=VMEM,
        scratch_shapes=scratch()
        + [
            pltpu.VMEM((len(pieces) * pieces[0].shape[0], BLOCK), jnp.bfloat16),
            pltpu.SemaphoreType.DMA((len(pieces),)),
        ],
        out_shape=jax.ShapeDtypeStruct((BLOCK, BLOCK), jnp.bfloat16),
        compiler_params=pltpu.CompilerParams(vmem_limit_bytes=VMEM_LIMIT),
        cost_estimate=pl.CostEstimate(
            flops=22 * BLOCK**3, bytes_accessed=4 * BLOCK**2, transcendentals=0
        ),
        name="value_inverse",
    )(place, *in_vmem(own_stats, other_stats), *in_hbm(*pieces))


def feature_kernel(core, table, counts, *refs, pieces, place, half_blocks, capacity):
    own_inverse, other_inverse = refs[2 * pieces], refs[2 * pieces + 1]
    out, state, halves, left, normed, cotangent, sems = refs[-7:]
    copies = row_copies(refs[:pieces], normed, sems)
    later = row_copies(refs[pieces : 2 * pieces], cotangent, sems, pieces)
    for copy in copies + later:
        copy.start()
    for copy in copies:
        copy.wait()
    owner = table[core[0] * half_blocks + place] // capacity
    inverse = inverse_of(normed[...], counts[owner], state, halves)
    for copy in later:
        copy.wait()
    grad = first_dim_product(normed[...], cotangent[...]).astype(jnp.bfloat16)
    left[...] = product(inverse, grad).astype(jnp.bfloat16)
    for turn, value_inverse in ((0, own_inverse), (1, other_inverse)):
        block = core[0] if turn == 0 else 1 - core[0]
        span = pl.ds(pl.multiple_of(block * BLOCK, BLOCK), BLOCK)
        out[:, span] = product(left[:, span], value_inverse[...]).astype(jnp.bfloat16)


def precondition(core, table, counts, normed, cotangents, inverses, place, half_blocks, capacity):
    value_width = cotangents[0].shape[1]
    pieces = len(normed)
    tokens = pieces * normed[0].shape[0]
    return pl.pallas_call(
        functools.partial(
            feature_kernel, pieces=pieces, place=place, half_blocks=half_blocks, capacity=capacity
        ),
        in_specs=[SMEM] * 3 + [HBM] * (2 * pieces) + [VMEM] * 2,
        out_specs=VMEM,
        scratch_shapes=scratch()
        + [
            pltpu.VMEM((BLOCK, value_width), jnp.bfloat16),
            pltpu.VMEM((tokens, BLOCK), jnp.bfloat16),
            pltpu.VMEM((tokens, value_width), jnp.bfloat16),
            pltpu.SemaphoreType.DMA((2 * pieces,)),
        ],
        out_shape=jax.ShapeDtypeStruct((BLOCK, value_width), jnp.bfloat16),
        compiler_params=pltpu.CompilerParams(vmem_limit_bytes=VMEM_LIMIT),
        cost_estimate=pl.CostEstimate(
            flops=34 * BLOCK**3, bytes_accessed=8 * BLOCK**2, transcendentals=0
        ),
        name="precondition",
    )(core, *in_hbm(table, counts, *normed, *cotangents), *in_vmem(*inverses))


def place_kernel(core, *refs, blocks):
    pieces, out, sems = refs[: 2 * blocks], refs[-2], refs[-1]
    copies = []
    for k, piece in enumerate(pieces):
        owner = core[0] if k < blocks else 1 - core[0]
        start = pl.multiple_of((owner * blocks + k % blocks) * BLOCK, BLOCK)
        copies.append(pltpu.make_async_copy(piece, out.at[pl.ds(start, BLOCK)], sems.at[k]))
    for copy in copies:
        copy.start()
    for copy in copies:
        copy.wait()


def place_rows(core, own, received):
    blocks = len(received)
    value_width = received[0].shape[1]
    return pl.pallas_call(
        functools.partial(place_kernel, blocks=blocks),
        in_specs=[SMEM] + [VMEM] * (2 * blocks),
        out_specs=HBM,
        out_shape=jax.ShapeDtypeStruct((2 * blocks * BLOCK, value_width), jnp.bfloat16),
        scratch_shapes=[pltpu.SemaphoreType.DMA((2 * blocks,))],
        compiler_params=pltpu.CompilerParams(vmem_limit_bytes=VMEM_LIMIT),
        cost_estimate=pl.CostEstimate(
            flops=0, bytes_accessed=8 * blocks * BLOCK * value_width, transcendentals=0
        ),
        name="place_rows",
    )(core, *in_vmem(*own, *received))


def placed_work(activations, norm_gain, weights, cotangent, top_grad, owner_slot, sweeps):
    acts, cot = activations[0], cotangent[0]
    table, counts = owner_slot[0, 0], sweeps[0, 0]
    _, half_width = acts.shape
    value_width = cot.shape[1]
    tensor_size = lax.axis_size("tensor")
    replica_count = lax.axis_size("dp")
    feature_blocks = half_width // BLOCK
    value_blocks = value_width // BLOCK
    unit_count = feature_blocks + 1 + feature_blocks * value_blocks
    capacity = (unit_count + replica_count - 1) // replica_count
    half_blocks = feature_blocks // 2
    core = (lax.axis_index("dp") % 2)[None]

    far = [cot]
    for bit in higher_bits("dp"):
        far = far + [flipped(piece, "dp", bit) for piece in far]
    cotangents = []
    for piece in far:
        cotangents += [piece, flipped(piece, "dp", 1)]

    scaled, own_stats = upstream_of(
        table, counts, cot, weights[0], acts, norm_gain, feature_blocks, capacity
    )
    other_stats = flipped(own_stats, "tensor", 1)
    term, first_sent, mine, theirs = terms_of(
        core, scaled, acts, norm_gain, own_stats, other_stats, half_width * tensor_size
    )
    arrived = relay(term, first_sent, "section")

    normed = []
    for own, sent in zip(mine, theirs):
        pieces = [own]
        for mask in range(1, replica_count):
            pieces.append(flipped(sent if mask % 2 else own, "dp", mask))
        normed.append(pieces)

    place = jnp.stack([core[0], lax.axis_index("tensor")])
    own_inverse = invert_value(place, own_stats, other_stats, cotangents)
    inverses = [own_inverse, flipped(own_inverse, "dp", 1)]

    own_rows, received = [], []
    for k in range(half_blocks):
        own_rows.append(
            precondition(
                core, table, counts, normed[k], cotangents, inverses, k, half_blocks, capacity
            )
        )
        received.append(flipped(own_rows[k], "dp", 1))
    output = place_rows(core, own_rows, received)
    section = lax.axis_index("section")[None]
    input_grad = finish(section, lax.axis_size("section"), top_grad, term, arrived)
    return (input_grad[None], output[None])


def solution(mesh):
    placed = (
        P("section", "dp", "tensor"),
        P("section", "tensor"),
        P("section", "tensor", None),
        P("section", "dp", None),
        P("dp", "tensor"),
        P("section", "tensor", None),
        P("section", "tensor", None),
    )
    return jax.shard_map(
        placed_work,
        mesh=mesh,
        in_specs=placed,
        out_specs=(P("section", "dp", "tensor"), P("section", "tensor", None)),
        check_vma=False,
    )
```

```python
import functools

import jax
import jax.numpy as jnp
from jax import lax
from jax.experimental import pallas as pl
from jax.experimental.pallas import tpu as pltpu
from jax.sharding import PartitionSpec as P


BLOCK = 512
EPSILON = 1e-05
DAMPING = 0.05
LANES = 128
STAT_ROWS = 8
RELAY_CHUNKS = 2
RELAY_LAG = 1
VMEM_LIMIT = 24 * 2**20


def flipped(value, axis, bit):
    count = lax.axis_size(axis)
    return lax.ppermute(value, axis, [(k, k ^ bit) for k in range(count)])


def higher_bits(axis):
    bit = 2
    while bit < lax.axis_size(axis):
        yield bit
        bit *= 2


def first_dim_product(left, right):
    return lax.dot_general(
        left, right, (((0,), (0,)), ((), ())), preferred_element_type=jnp.float32
    )


def product(left, right):
    return jnp.dot(left, right, preferred_element_type=jnp.float32)


def inverse_of(tokens, limit, state, halves):
    count, order = tokens.shape
    rows = lax.broadcasted_iota(jnp.int32, (order, order), 0)
    columns = lax.broadcasted_iota(jnp.int32, (order, order), 1)
    diagonal = rows == columns
    matrix = first_dim_product(tokens, tokens) * (1.0 / count)
    matrix = matrix + jnp.where(diagonal, DAMPING, 0.0)
    scale = lax.rsqrt(jnp.sum(matrix * matrix))
    first = matrix * scale
    start = jnp.where(diagonal, 2.0, 0.0) - first
    first_half = first.astype(jnp.bfloat16)
    state[0] = start
    halves[0:order] = start.astype(jnp.bfloat16)
    grown = 2.0 * first - product(first_half, first_half)
    state[1] = grown
    halves[order:] = grown.astype(jnp.bfloat16)

    def sweep(k, carry):
        change = product(halves[...], halves[order:])
        approx = 2.0 * state[0] - change[:order]
        grown = 2.0 * state[1] - change[order:]
        state[0] = approx
        state[1] = grown
        halves[0:order] = approx.astype(jnp.bfloat16)
        halves[order:] = grown.astype(jnp.bfloat16)
        return carry

    lax.fori_loop(2, limit, sweep, 0)
    last = 2.0 * state[0] - product(halves[0:order], halves[order:])
    return (last * scale).astype(jnp.bfloat16)


def upstream_kernel(
    table, counts, cot_hbm, weight_hbm, act_hbm, gain_hbm, scaled_ref, stats_ref, cot, weight, act, gain, sems, *, position, capacity
):
    tokens, width = act.shape
    blocks = width // BLOCK
    small = [
        pltpu.make_async_copy(source, target, sems.at[k])
        for k, (source, target) in enumerate(((act_hbm, act), (cot_hbm, cot), (gain_hbm, gain)))
    ]
    large = [
        pltpu.make_async_copy(
            weight_hbm.at[pl.ds(k * BLOCK, BLOCK)],
            weight.at[pl.ds(k * BLOCK, BLOCK)],
            sems.at[3 + k],
        )
        for k in range(blocks)
    ]
    for copy in small + large:
        copy.start()
    small[0].wait()
    squares = jnp.zeros((tokens, LANES), jnp.float32)
    for k in range(width // LANES):
        inputs = act[:, k * LANES : (k + 1) * LANES].astype(jnp.float32)
        squares += inputs * inputs
    limit = counts[table[position] // capacity].astype(jnp.float32)
    stats_ref[...] = jnp.full(stats_ref.shape, limit, jnp.float32)
    stats_ref[0:1] = jnp.sum(squares.T, axis=0, keepdims=True)
    small[1].wait()
    small[2].wait()
    inner = jnp.zeros((tokens, LANES), jnp.float32)
    for k in range(blocks):
        span = slice(k * BLOCK, (k + 1) * BLOCK)
        large[k].wait()
        upstream = lax.dot_general(
            cot[...], weight[span], (((1,), (1,)), ((), ())), preferred_element_type=jnp.float32
        )
        scaled = upstream * gain[:, span]
        scaled_ref[:, span] = scaled
        for j in range(BLOCK // LANES):
            lanes = slice(j * LANES, (j + 1) * LANES)
            start = k * BLOCK + j * LANES
            inner += scaled[:, lanes] * act[:, start : start + LANES].astype(jnp.float32)
    stats_ref[1:2] = jnp.sum(inner.T, axis=0, keepdims=True)


SMEM = pl.BlockSpec(memory_space=pltpu.SMEM)
VMEM = pl.BlockSpec(memory_space=pltpu.VMEM)
HBM = pl.BlockSpec(memory_space=pltpu.HBM)
ANY = pl.BlockSpec(memory_space=pl.ANY)


def in_hbm(*arrays):
    return [pltpu.with_memory_space_constraint(array, pltpu.HBM) for array in arrays]


def in_vmem(*arrays):
    return [pltpu.with_memory_space_constraint(array, pltpu.VMEM) for array in arrays]


def upstream_of(table, counts, cotangent, weights, activations, gain, position, capacity):
    tokens, value_width = cotangent.shape
    width = weights.shape[0]
    return pl.pallas_call(
        functools.partial(upstream_kernel, position=position, capacity=capacity),
        in_specs=[SMEM, SMEM, HBM, HBM, HBM, HBM],
        out_specs=[VMEM, VMEM],
        out_shape=[
            jax.ShapeDtypeStruct((tokens, width), jnp.float32),
            jax.ShapeDtypeStruct((STAT_ROWS, tokens), jnp.float32),
        ],
        scratch_shapes=[
            pltpu.VMEM(cotangent.shape, cotangent.dtype),
            pltpu.VMEM(weights.shape, weights.dtype),
            pltpu.VMEM(activations.shape, activations.dtype),
            pltpu.VMEM(gain.shape, gain.dtype),
            pltpu.SemaphoreType.DMA((3 + width // BLOCK,)),
        ],
        compiler_params=pltpu.CompilerParams(vmem_limit_bytes=VMEM_LIMIT),
        cost_estimate=pl.CostEstimate(
            flops=2 * tokens * width * value_width,
            bytes_accessed=2 * width * value_width + 8 * tokens * width,
            transcendentals=0,
        ),
        name="upstream",
    )(*in_hbm(table, counts, cotangent, weights, activations, gain))


def column(row):
    return jnp.broadcast_to(row, (LANES, row.shape[1])).T[:, :1]


def terms_kernel(core, scaled_ref, act_ref, gain_ref, own_ref, other_ref, term_ref, *refs, full_width):
    normed, first_sent, pieces = refs[-1], refs[-2], refs[:-2]
    squares = own_ref[0:1] + other_ref[0:1]
    inner_sum = own_ref[1:2] + other_ref[1:2]
    inverse_rms = lax.rsqrt(squares * (1.0 / full_width) + EPSILON)
    coefficient = inverse_rms * inverse_rms * inverse_rms * inner_sum * (1.0 / full_width)
    inverse_rms, coefficient = column(inverse_rms), column(coefficient)
    inputs = act_ref[...].astype(jnp.float32)
    normed[...] = (inputs * inverse_rms * gain_ref[...]).astype(jnp.bfloat16)
    term = inverse_rms * scaled_ref[...] - inputs * coefficient
    term_ref[...] = term.astype(jnp.bfloat16)
    first_sent[...] = term[: first_sent.shape[0]].astype(jnp.bfloat16)
    half = normed.shape[1] // 2
    blocks = half // BLOCK
    for k in range(blocks):
        mine = pl.multiple_of(core[0] * half + k * BLOCK, BLOCK)
        theirs = pl.multiple_of((1 - core[0]) * half + k * BLOCK, BLOCK)
        pieces[k][...] = normed[:, pl.ds(mine, BLOCK)]
        pieces[blocks + k][...] = normed[:, pl.ds(theirs, BLOCK)]


def terms_of(core, scaled, activations, gain, own_stats, other_stats, full_width):
    tokens, width = scaled.shape
    blocks = width // BLOCK
    smem = pl.BlockSpec(memory_space=pltpu.SMEM)
    vmem = pl.BlockSpec(memory_space=pltpu.VMEM)
    outs = pl.pallas_call(
        functools.partial(terms_kernel, full_width=full_width),
        in_specs=[smem] + [vmem] * 5,
        out_specs=[vmem] * (2 + blocks),
        out_shape=[jax.ShapeDtypeStruct((tokens, width), jnp.bfloat16)]
        + [jax.ShapeDtypeStruct((tokens, BLOCK), jnp.bfloat16)] * blocks
        + [jax.ShapeDtypeStruct((tokens // RELAY_CHUNKS, width), jnp.bfloat16)],
        scratch_shapes=[pltpu.VMEM((tokens, width), jnp.bfloat16)],
        compiler_params=pltpu.CompilerParams(vmem_limit_bytes=VMEM_LIMIT),
        cost_estimate=pl.CostEstimate(
            flops=8 * tokens * width, bytes_accessed=10 * tokens * width, transcendentals=0
        ),
        name="terms",
    )(core, *in_vmem(scaled, activations, gain, own_stats, other_stats))
    return outs[0], outs[-1], outs[1 : 1 + blocks // 2], outs[1 + blocks // 2 : -1]


def payload_kernel(section, term, arrived, out, *, wave, sections):
    rows = out.shape[0]
    chunk = wave - RELAY_LAG * (sections - 1 - section[0])
    chunk = jnp.minimum(jnp.maximum(chunk, 0), RELAY_CHUNKS - 1)
    own = term[pl.ds(pl.multiple_of(chunk * rows, rows), rows)].astype(jnp.float32)
    out[...] = (own + arrived[...].astype(jnp.float32)).astype(jnp.bfloat16)


def payload(section, term, arrived, wave, sections):
    return pl.pallas_call(
        functools.partial(payload_kernel, wave=wave, sections=sections),
        in_specs=[SMEM, VMEM, VMEM],
        out_specs=VMEM,
        out_shape=jax.ShapeDtypeStruct(arrived.shape, jnp.bfloat16),
        compiler_params=pltpu.CompilerParams(vmem_limit_bytes=VMEM_LIMIT),
        cost_estimate=pl.CostEstimate(
            flops=arrived.size, bytes_accessed=6 * arrived.size, transcendentals=0
        ),
        name="payload",
    )(section, *in_vmem(term, arrived))


def relay(term, first_sent, section, axis):
    count = lax.axis_size(axis)
    arrived = []
    for wave in range(RELAY_CHUNKS + RELAY_LAG * (count - 2)):
        sent = first_sent
        if wave >= RELAY_LAG:
            sent = payload(section, term, arrived[wave - RELAY_LAG], wave, count)
        pairs = [(k, k - 1) for k in range(1, count)]
        arrived.append(lax.ppermute(sent, axis, pairs))
    return arrived


def finish_kernel(section, top_ref, term_ref, *refs, sections):
    arrived, out = refs[:-1], refs[-1]
    rows = arrived[0].shape[0]
    for chunk in range(RELAY_CHUNKS):
        span = slice(chunk * rows, (chunk + 1) * rows)
        own = top_ref[span].astype(jnp.float32) + term_ref[span].astype(jnp.float32)

        @pl.when(section[0] == sections - 1)
        def _(span=span, own=own):
            out[span] = own.astype(jnp.bfloat16)

        for place in range(sections - 1):
            later = arrived[chunk + RELAY_LAG * (sections - 2 - place)]

            @pl.when(section[0] == place)
            def _(span=span, own=own, later=later):
                out[span] = (own + later[...].astype(jnp.float32)).astype(jnp.bfloat16)


def finish(section, sections, top_grad, term, arrived):
    vmem = pl.BlockSpec(memory_space=pltpu.VMEM)
    return pl.pallas_call(
        functools.partial(finish_kernel, sections=sections),
        in_specs=[pl.BlockSpec(memory_space=pltpu.SMEM)] + [vmem] * (2 + len(arrived)),
        out_specs=vmem,
        out_shape=jax.ShapeDtypeStruct(term.shape, jnp.bfloat16),
        compiler_params=pltpu.CompilerParams(vmem_limit_bytes=VMEM_LIMIT),
        cost_estimate=pl.CostEstimate(
            flops=2 * term.size, bytes_accessed=8 * term.size, transcendentals=0
        ),
        name="finish",
    )(section, *in_vmem(top_grad, term, *arrived))


def scratch():
    return [
        pltpu.VMEM((2, BLOCK, BLOCK), jnp.float32),
        pltpu.VMEM((2 * BLOCK, BLOCK), jnp.bfloat16),
    ]


def value_kernel(core, tensor, own_stats, other_stats, *refs, pieces):
    span = pl.ds(pl.multiple_of(core[0] * BLOCK, BLOCK), BLOCK)
    tokens = jnp.concatenate([ref[:, span] for ref in refs[:pieces]], axis=0)
    out, state, halves = refs[pieces:]
    own_limit, other_limit = jnp.max(own_stats[2:3]), jnp.max(other_stats[2:3])
    limit = jnp.where(core[0] == tensor[0], own_limit, other_limit).astype(jnp.int32)
    out[...] = inverse_of(tokens, limit, state, halves)


def invert_value(core, tensor, own_stats, other_stats, pieces):
    return pl.pallas_call(
        functools.partial(value_kernel, pieces=len(pieces)),
        in_specs=[SMEM, SMEM] + [VMEM] * (2 + len(pieces)),
        out_specs=VMEM,
        scratch_shapes=scratch(),
        out_shape=jax.ShapeDtypeStruct((BLOCK, BLOCK), jnp.bfloat16),
        compiler_params=pltpu.CompilerParams(vmem_limit_bytes=VMEM_LIMIT),
        cost_estimate=pl.CostEstimate(
            flops=22 * BLOCK**3, bytes_accessed=4 * BLOCK**2, transcendentals=0
        ),
        name="value_inverse",
    )(core, tensor, *in_vmem(own_stats, other_stats, *pieces))


def feature_kernel(core, table, counts, *refs, pieces, place, half_blocks, capacity):
    normed = jnp.concatenate([ref[...] for ref in refs[:pieces]], axis=0)
    own_inverse, other_inverse = refs[2 * pieces], refs[2 * pieces + 1]
    out, state, halves, left = refs[-4:]
    owner = table[core[0] * half_blocks + place] // capacity
    inverse = inverse_of(normed, counts[owner], state, halves)
    cotangent = jnp.concatenate([ref[...] for ref in refs[pieces : 2 * pieces]], axis=0)
    grad = first_dim_product(normed, cotangent).astype(jnp.bfloat16)
    left[...] = product(inverse, grad).astype(jnp.bfloat16)
    for turn, value_inverse in ((0, own_inverse), (1, other_inverse)):
        block = core[0] if turn == 0 else 1 - core[0]
        span = pl.ds(pl.multiple_of(block * BLOCK, BLOCK), BLOCK)
        out[:, span] = product(left[:, span], value_inverse[...]).astype(jnp.bfloat16)


def precondition(core, table, counts, normed, cotangents, inverses, place, half_blocks, capacity):
    value_width = cotangents[0].shape[1]
    pieces = len(normed)
    return pl.pallas_call(
        functools.partial(
            feature_kernel, pieces=pieces, place=place, half_blocks=half_blocks, capacity=capacity
        ),
        in_specs=[SMEM] * 3 + [VMEM] * (2 * pieces + 2),
        out_specs=VMEM,
        scratch_shapes=scratch() + [pltpu.VMEM((BLOCK, value_width), jnp.bfloat16)],
        out_shape=jax.ShapeDtypeStruct((BLOCK, value_width), jnp.bfloat16),
        compiler_params=pltpu.CompilerParams(vmem_limit_bytes=VMEM_LIMIT),
        cost_estimate=pl.CostEstimate(
            flops=34 * BLOCK**3, bytes_accessed=8 * BLOCK**2, transcendentals=0
        ),
        name="precondition",
    )(core, *in_hbm(table, counts), *in_vmem(*normed, *cotangents, *inverses))


def place_kernel(core, *refs, blocks):
    pieces, out, sems = refs[: 2 * blocks], refs[-2], refs[-1]
    copies = []
    for k, piece in enumerate(pieces):
        owner = core[0] if k < blocks else 1 - core[0]
        start = pl.multiple_of((owner * blocks + k % blocks) * BLOCK, BLOCK)
        copies.append(pltpu.make_async_copy(piece, out.at[pl.ds(start, BLOCK)], sems.at[k]))
    for copy in copies:
        copy.start()
    for copy in copies:
        copy.wait()


def place_rows(core, own, received):
    blocks = len(received)
    value_width = received[0].shape[1]
    return pl.pallas_call(
        functools.partial(place_kernel, blocks=blocks),
        in_specs=[SMEM] + [VMEM] * (2 * blocks),
        out_specs=HBM,
        out_shape=jax.ShapeDtypeStruct((2 * blocks * BLOCK, value_width), jnp.bfloat16),
        scratch_shapes=[pltpu.SemaphoreType.DMA((2 * blocks,))],
        compiler_params=pltpu.CompilerParams(vmem_limit_bytes=VMEM_LIMIT),
        cost_estimate=pl.CostEstimate(
            flops=0, bytes_accessed=8 * blocks * BLOCK * value_width, transcendentals=0
        ),
        name="place_rows",
    )(core, *in_vmem(*own, *received))


def placed_work(activations, norm_gain, weights, cotangent, top_grad, owner_slot, sweeps):
    acts, cot = activations[0], cotangent[0]
    table, counts = owner_slot[0, 0], sweeps[0, 0]
    _, half_width = acts.shape
    value_width = cot.shape[1]
    tensor_size = lax.axis_size("tensor")
    replica_count = lax.axis_size("dp")
    feature_blocks = half_width // BLOCK
    value_blocks = value_width // BLOCK
    unit_count = feature_blocks + 1 + feature_blocks * value_blocks
    capacity = (unit_count + replica_count - 1) // replica_count
    half_blocks = feature_blocks // 2
    core = (lax.axis_index("dp") % 2)[None]

    far = [cot]
    for bit in higher_bits("dp"):
        far = far + [flipped(piece, "dp", bit) for piece in far]
    cotangents = []
    for piece in far:
        cotangents += [piece, flipped(piece, "dp", 1)]

    scaled, own_stats = upstream_of(
        table, counts, cot, weights[0], acts, norm_gain, feature_blocks, capacity
    )
    other_stats = flipped(own_stats, "tensor", 1)
    term, first_sent, mine, theirs = terms_of(
        core, scaled, acts, norm_gain, own_stats, other_stats, half_width * tensor_size
    )
    section = lax.axis_index("section")[None]
    arrived = relay(term, first_sent, section, "section")

    normed = []
    for own, sent in zip(mine, theirs):
        pieces = [own]
        for mask in range(1, replica_count):
            pieces.append(flipped(sent if mask % 2 else own, "dp", mask))
        normed.append(pieces)

    tensor = lax.axis_index("tensor")[None]
    own_inverse = invert_value(core, tensor, own_stats, other_stats, cotangents)
    inverses = [own_inverse, flipped(own_inverse, "dp", 1)]

    own_rows, received = [], []
    for k in range(half_blocks):
        own_rows.append(
            precondition(
                core, table, counts, normed[k], cotangents, inverses, k, half_blocks, capacity
            )
        )
        received.append(flipped(own_rows[k], "dp", 1))
    output = place_rows(core, own_rows, received)
    input_grad = finish(section, lax.axis_size("section"), top_grad, term, arrived)
    return (input_grad[None], output[None])


def solution(mesh):
    placed = (
        P("section", "dp", "tensor"),
        P("section", "tensor"),
        P("section", "tensor", None),
        P("section", "dp", None),
        P("dp", "tensor"),
        P("section", "tensor", None),
        P("section", "tensor", None),
    )
    return jax.shard_map(
        placed_work,
        mesh=mesh,
        in_specs=placed,
        out_specs=(P("section", "dp", "tensor"), P("section", "tensor", None)),
        check_vma=False,
    )
```

```python
import functools

import jax
import jax.numpy as jnp
from jax import lax
from jax.experimental import pallas as pl
from jax.experimental.pallas import tpu as pltpu
from jax.sharding import PartitionSpec as P


BLOCK = 512
EPSILON = 1e-05
DAMPING = 0.05
LANES = 128
STAT_ROWS = 8
RELAY_CHUNKS = 2
RELAY_LAG = 1
VMEM_LIMIT = 24 * 2**20


def flipped(value, axis, bit):
    count = lax.axis_size(axis)
    return lax.ppermute(value, axis, [(k, k ^ bit) for k in range(count)])


def higher_bits(axis):
    bit = 2
    while bit < lax.axis_size(axis):
        yield bit
        bit *= 2


def first_dim_product(left, right):
    return lax.dot_general(
        left, right, (((0,), (0,)), ((), ())), preferred_element_type=jnp.float32
    )


def product(left, right):
    return jnp.dot(left, right, preferred_element_type=jnp.float32)


def inverse_of(tokens, limit, state, halves):
    count, order = tokens.shape
    rows = lax.broadcasted_iota(jnp.int32, (order, order), 0)
    columns = lax.broadcasted_iota(jnp.int32, (order, order), 1)
    diagonal = rows == columns
    matrix = first_dim_product(tokens, tokens) * (1.0 / count)
    matrix = matrix + jnp.where(diagonal, DAMPING, 0.0)
    state[0] = matrix
    halves[0:order] = matrix.astype(jnp.bfloat16)
    square = product(halves[0:order], halves[0:order])
    scale = lax.rsqrt(jnp.sum(matrix * matrix))
    first = state[0] * scale
    grown = 2.0 * first - (scale * scale) * square
    start = jnp.where(diagonal, 2.0, 0.0) - first
    state[0] = start
    state[1] = grown
    halves[0:order] = start.astype(jnp.bfloat16)
    halves[order:] = grown.astype(jnp.bfloat16)

    def sweep(k, carry):
        change = product(halves[...], halves[order:])
        approx = 2.0 * state[0] - change[:order]
        grown = 2.0 * state[1] - change[order:]
        state[0] = approx
        state[1] = grown
        halves[0:order] = approx.astype(jnp.bfloat16)
        halves[order:] = grown.astype(jnp.bfloat16)
        return carry

    lax.fori_loop(2, limit, sweep, 0)
    last = 2.0 * state[0] - product(halves[0:order], halves[order:])
    return (last * scale).astype(jnp.bfloat16)


def upstream_kernel(
    table, counts, cot_hbm, weight_hbm, act_hbm, gain_hbm, scaled_ref, stats_ref, act, gain, cot, weight, sems, *, position, capacity
):
    tokens, width = act.shape
    size = BLOCK
    blocks = width // size
    small = [
        pltpu.make_async_copy(source, target, sems.at[k])
        for k, (source, target) in enumerate(((act_hbm, act), (cot_hbm, cot), (gain_hbm, gain)))
    ]
    large = [
        pltpu.make_async_copy(
            weight_hbm.at[pl.ds(k * size, size)],
            weight.at[pl.ds(k * size, size)],
            sems.at[3 + k],
        )
        for k in range(blocks)
    ]
    for copy in small + large:
        copy.start()
    small[0].wait()
    squares = jnp.zeros((tokens, LANES), jnp.float32)
    for k in range(width // LANES):
        inputs = act[:, k * LANES : (k + 1) * LANES].astype(jnp.float32)
        squares += inputs * inputs
    limit = counts[table[position] // capacity].astype(jnp.float32)
    stats_ref[...] = jnp.full(stats_ref.shape, limit, jnp.float32)
    stats_ref[0:1] = jnp.sum(squares.T, axis=0, keepdims=True)
    small[1].wait()
    small[2].wait()
    inner = jnp.zeros((tokens, LANES), jnp.float32)
    for k in range(blocks):
        span = slice(k * size, (k + 1) * size)
        large[k].wait()
        upstream = lax.dot_general(
            cot[...], weight[span], (((1,), (1,)), ((), ())), preferred_element_type=jnp.float32
        )
        scaled = upstream * gain[:, span]
        scaled_ref[:, span] = scaled
        for j in range(size // LANES):
            lanes = slice(j * LANES, (j + 1) * LANES)
            start = k * size + j * LANES
            inner += scaled[:, lanes] * act[:, start : start + LANES].astype(jnp.float32)
    stats_ref[1:2] = jnp.sum(inner.T, axis=0, keepdims=True)


SMEM = pl.BlockSpec(memory_space=pltpu.SMEM)
VMEM = pl.BlockSpec(memory_space=pltpu.VMEM)
HBM = pl.BlockSpec(memory_space=pltpu.HBM)
ANY = pl.BlockSpec(memory_space=pl.ANY)


def in_hbm(*arrays):
    return [pltpu.with_memory_space_constraint(array, pltpu.HBM) for array in arrays]


def in_vmem(*arrays):
    return [pltpu.with_memory_space_constraint(array, pltpu.VMEM) for array in arrays]


def upstream_of(table, counts, cotangent, weights, activations, gain, position, capacity):
    tokens, value_width = cotangent.shape
    width = weights.shape[0]
    return pl.pallas_call(
        functools.partial(upstream_kernel, position=position, capacity=capacity),
        in_specs=[SMEM, SMEM, HBM, HBM, HBM, HBM],
        out_specs=[VMEM] * 4,
        out_shape=[
            jax.ShapeDtypeStruct((tokens, width), jnp.float32),
            jax.ShapeDtypeStruct((STAT_ROWS, tokens), jnp.float32),
            jax.ShapeDtypeStruct(activations.shape, activations.dtype),
            jax.ShapeDtypeStruct(gain.shape, gain.dtype),
        ],
        scratch_shapes=[
            pltpu.VMEM(cotangent.shape, cotangent.dtype),
            pltpu.VMEM(weights.shape, weights.dtype),
            pltpu.SemaphoreType.DMA((3 + width // BLOCK,)),
        ],
        compiler_params=pltpu.CompilerParams(vmem_limit_bytes=VMEM_LIMIT),
        cost_estimate=pl.CostEstimate(
            flops=2 * tokens * width * value_width,
            bytes_accessed=2 * width * value_width + 8 * tokens * width,
            transcendentals=0,
        ),
        name="upstream",
    )(*in_hbm(table, counts, cotangent, weights, activations, gain))


def column(row):
    return jnp.broadcast_to(row, (LANES, row.shape[1])).T[:, :1]


def terms_kernel(core, scaled_ref, act_ref, gain_ref, own_ref, other_ref, term_ref, *refs, full_width):
    normed, first_sent, pieces = refs[-1], refs[-2], refs[:-2]
    squares = own_ref[0:1] + other_ref[0:1]
    inner_sum = own_ref[1:2] + other_ref[1:2]
    inverse_rms = lax.rsqrt(squares * (1.0 / full_width) + EPSILON)
    coefficient = inverse_rms * inverse_rms * inverse_rms * inner_sum * (1.0 / full_width)
    inverse_rms, coefficient = column(inverse_rms), column(coefficient)
    inputs = act_ref[...].astype(jnp.float32)
    normed[...] = (inputs * inverse_rms * gain_ref[...]).astype(jnp.bfloat16)
    term = inverse_rms * scaled_ref[...] - inputs * coefficient
    term_ref[...] = term.astype(jnp.bfloat16)
    first_sent[...] = term[: first_sent.shape[0]].astype(jnp.bfloat16)
    half = normed.shape[1] // 2
    blocks = half // BLOCK
    for k in range(blocks):
        mine = pl.multiple_of(core[0] * half + k * BLOCK, BLOCK)
        theirs = pl.multiple_of((1 - core[0]) * half + k * BLOCK, BLOCK)
        pieces[k][...] = normed[:, pl.ds(mine, BLOCK)]
        pieces[blocks + k][...] = normed[:, pl.ds(theirs, BLOCK)]


def terms_of(core, scaled, activations, gain, own_stats, other_stats, full_width):
    tokens, width = scaled.shape
    blocks = width // BLOCK
    smem = pl.BlockSpec(memory_space=pltpu.SMEM)
    vmem = pl.BlockSpec(memory_space=pltpu.VMEM)
    outs = pl.pallas_call(
        functools.partial(terms_kernel, full_width=full_width),
        in_specs=[smem] + [vmem] * 5,
        out_specs=[vmem] * (2 + blocks),
        out_shape=[jax.ShapeDtypeStruct((tokens, width), jnp.bfloat16)]
        + [jax.ShapeDtypeStruct((tokens, BLOCK), jnp.bfloat16)] * blocks
        + [jax.ShapeDtypeStruct((tokens // RELAY_CHUNKS, width), jnp.bfloat16)],
        scratch_shapes=[pltpu.VMEM((tokens, width), jnp.bfloat16)],
        compiler_params=pltpu.CompilerParams(vmem_limit_bytes=VMEM_LIMIT),
        cost_estimate=pl.CostEstimate(
            flops=8 * tokens * width, bytes_accessed=10 * tokens * width, transcendentals=0
        ),
        name="terms",
    )(core, *in_vmem(scaled, activations, gain, own_stats, other_stats))
    return outs[0], outs[-1], outs[1 : 1 + blocks // 2], outs[1 + blocks // 2 : -1]


def payload_kernel(section, term, arrived, out, *, wave, sections):
    rows = out.shape[0]
    chunk = wave - RELAY_LAG * (sections - 1 - section[0])
    chunk = jnp.minimum(jnp.maximum(chunk, 0), RELAY_CHUNKS - 1)
    own = term[pl.ds(pl.multiple_of(chunk * rows, rows), rows)].astype(jnp.float32)
    out[...] = (own + arrived[...].astype(jnp.float32)).astype(jnp.bfloat16)


def payload(section, term, arrived, wave, sections):
    return pl.pallas_call(
        functools.partial(payload_kernel, wave=wave, sections=sections),
        in_specs=[SMEM, VMEM, VMEM],
        out_specs=VMEM,
        out_shape=jax.ShapeDtypeStruct(arrived.shape, jnp.bfloat16),
        compiler_params=pltpu.CompilerParams(vmem_limit_bytes=VMEM_LIMIT),
        cost_estimate=pl.CostEstimate(
            flops=arrived.size, bytes_accessed=6 * arrived.size, transcendentals=0
        ),
        name="payload",
    )(section, *in_vmem(term, arrived))


def relay(term, first_sent, section, axis):
    count = lax.axis_size(axis)
    arrived = []
    for wave in range(RELAY_CHUNKS + RELAY_LAG * (count - 2)):
        sent = first_sent
        if wave >= RELAY_LAG:
            sent = payload(section, term, arrived[wave - RELAY_LAG], wave, count)
        pairs = [
            (k, k - 1)
            for k in range(1, count)
            if 0 <= wave - RELAY_LAG * (count - 1 - k) < RELAY_CHUNKS
        ]
        arrived.append(lax.ppermute(sent, axis, pairs))
    return arrived


def finish_kernel(section, top_ref, term_ref, *refs, sections):
    arrived, out = refs[:-1], refs[-1]
    rows = arrived[0].shape[0]
    for chunk in range(RELAY_CHUNKS):
        span = slice(chunk * rows, (chunk + 1) * rows)
        own = top_ref[span].astype(jnp.float32) + term_ref[span].astype(jnp.float32)

        @pl.when(section[0] == sections - 1)
        def _(span=span, own=own):
            out[span] = own.astype(jnp.bfloat16)

        for place in range(sections - 1):
            later = arrived[chunk + RELAY_LAG * (sections - 2 - place)]

            @pl.when(section[0] == place)
            def _(span=span, own=own, later=later):
                out[span] = (own + later[...].astype(jnp.float32)).astype(jnp.bfloat16)


def finish(section, sections, top_grad, term, arrived):
    vmem = pl.BlockSpec(memory_space=pltpu.VMEM)
    return pl.pallas_call(
        functools.partial(finish_kernel, sections=sections),
        in_specs=[pl.BlockSpec(memory_space=pltpu.SMEM)] + [vmem] * (2 + len(arrived)),
        out_specs=vmem,
        out_shape=jax.ShapeDtypeStruct(term.shape, jnp.bfloat16),
        compiler_params=pltpu.CompilerParams(vmem_limit_bytes=VMEM_LIMIT),
        cost_estimate=pl.CostEstimate(
            flops=2 * term.size, bytes_accessed=8 * term.size, transcendentals=0
        ),
        name="finish",
    )(section, *in_vmem(top_grad, term, *arrived))


def scratch():
    return [
        pltpu.VMEM((2, BLOCK, BLOCK), jnp.float32),
        pltpu.VMEM((2 * BLOCK, BLOCK), jnp.bfloat16),
    ]


def value_kernel(core, tensor, own_stats, other_stats, *refs, pieces):
    span = pl.ds(pl.multiple_of(core[0] * BLOCK, BLOCK), BLOCK)
    tokens = jnp.concatenate([ref[:, span] for ref in refs[:pieces]], axis=0)
    out, state, halves = refs[pieces:]
    own_limit, other_limit = jnp.max(own_stats[2:3]), jnp.max(other_stats[2:3])
    limit = jnp.where(core[0] == tensor[0], own_limit, other_limit).astype(jnp.int32)
    out[...] = inverse_of(tokens, limit, state, halves)


def invert_value(core, tensor, own_stats, other_stats, pieces):
    return pl.pallas_call(
        functools.partial(value_kernel, pieces=len(pieces)),
        in_specs=[SMEM, SMEM] + [VMEM] * (2 + len(pieces)),
        out_specs=VMEM,
        scratch_shapes=scratch(),
        out_shape=jax.ShapeDtypeStruct((BLOCK, BLOCK), jnp.bfloat16),
        compiler_params=pltpu.CompilerParams(vmem_limit_bytes=VMEM_LIMIT),
        cost_estimate=pl.CostEstimate(
            flops=22 * BLOCK**3, bytes_accessed=4 * BLOCK**2, transcendentals=0
        ),
        name="value_inverse",
    )(core, tensor, *in_vmem(own_stats, other_stats, *pieces))


def feature_kernel(core, table, counts, *refs, pieces, place, half_blocks, capacity):
    normed = jnp.concatenate([ref[...] for ref in refs[:pieces]], axis=0)
    own_inverse, other_inverse = refs[2 * pieces], refs[2 * pieces + 1]
    out, state, halves, left = refs[-4:]
    owner = table[core[0] * half_blocks + place] // capacity
    inverse = inverse_of(normed, counts[owner], state, halves)
    cotangent = jnp.concatenate([ref[...] for ref in refs[pieces : 2 * pieces]], axis=0)
    grad = first_dim_product(normed, cotangent).astype(jnp.bfloat16)
    left[...] = product(inverse, grad).astype(jnp.bfloat16)
    for turn, value_inverse in ((0, own_inverse), (1, other_inverse)):
        block = core[0] if turn == 0 else 1 - core[0]
        span = pl.ds(pl.multiple_of(block * BLOCK, BLOCK), BLOCK)
        out[:, span] = product(left[:, span], value_inverse[...]).astype(jnp.bfloat16)


def precondition(core, table, counts, normed, cotangents, inverses, place, half_blocks, capacity):
    value_width = cotangents[0].shape[1]
    pieces = len(normed)
    return pl.pallas_call(
        functools.partial(
            feature_kernel, pieces=pieces, place=place, half_blocks=half_blocks, capacity=capacity
        ),
        in_specs=[SMEM] * 3 + [VMEM] * (2 * pieces + 2),
        out_specs=VMEM,
        scratch_shapes=scratch() + [pltpu.VMEM((BLOCK, value_width), jnp.bfloat16)],
        out_shape=jax.ShapeDtypeStruct((BLOCK, value_width), jnp.bfloat16),
        compiler_params=pltpu.CompilerParams(vmem_limit_bytes=VMEM_LIMIT),
        cost_estimate=pl.CostEstimate(
            flops=34 * BLOCK**3, bytes_accessed=8 * BLOCK**2, transcendentals=0
        ),
        name="precondition",
    )(core, *in_hbm(table, counts), *in_vmem(*normed, *cotangents, *inverses))


def place_kernel(core, *refs, blocks):
    pieces, out, sems = refs[: 2 * blocks], refs[-2], refs[-1]
    copies = []
    for k, piece in enumerate(pieces):
        owner = core[0] if k < blocks else 1 - core[0]
        start = pl.multiple_of((owner * blocks + k % blocks) * BLOCK, BLOCK)
        copies.append(pltpu.make_async_copy(piece, out.at[pl.ds(start, BLOCK)], sems.at[k]))
    for copy in copies:
        copy.start()
    for copy in copies:
        copy.wait()


def place_rows(core, own, received):
    blocks = len(received)
    value_width = received[0].shape[1]
    return pl.pallas_call(
        functools.partial(place_kernel, blocks=blocks),
        in_specs=[SMEM] + [VMEM] * (2 * blocks),
        out_specs=HBM,
        out_shape=jax.ShapeDtypeStruct((2 * blocks * BLOCK, value_width), jnp.bfloat16),
        scratch_shapes=[pltpu.SemaphoreType.DMA((2 * blocks,))],
        compiler_params=pltpu.CompilerParams(vmem_limit_bytes=VMEM_LIMIT),
        cost_estimate=pl.CostEstimate(
            flops=0, bytes_accessed=8 * blocks * BLOCK * value_width, transcendentals=0
        ),
        name="place_rows",
    )(core, *in_vmem(*own, *received))


def placed_work(activations, norm_gain, weights, cotangent, top_grad, owner_slot, sweeps):
    acts, cot = activations[0], cotangent[0]
    table, counts = owner_slot[0, 0], sweeps[0, 0]
    _, half_width = acts.shape
    value_width = cot.shape[1]
    tensor_size = lax.axis_size("tensor")
    replica_count = lax.axis_size("dp")
    feature_blocks = half_width // BLOCK
    value_blocks = value_width // BLOCK
    unit_count = feature_blocks + 1 + feature_blocks * value_blocks
    capacity = (unit_count + replica_count - 1) // replica_count
    half_blocks = feature_blocks // 2
    core = (lax.axis_index("dp") % 2)[None]

    far = [cot]
    for bit in higher_bits("dp"):
        far = far + [flipped(piece, "dp", bit) for piece in far]
    cotangents = []
    for piece in far:
        cotangents += [piece, flipped(piece, "dp", 1)]

    scaled, own_stats, local_acts, local_gain = upstream_of(
        table, counts, cot, weights[0], acts, norm_gain, feature_blocks, capacity
    )
    other_stats = flipped(own_stats, "tensor", 1)
    term, first_sent, mine, theirs = terms_of(
        core, scaled, local_acts, local_gain, own_stats, other_stats, half_width * tensor_size
    )
    section = lax.axis_index("section")[None]
    arrived = relay(term, first_sent, section, "section")

    normed = []
    for own, sent in zip(mine, theirs):
        pieces = [own]
        for mask in range(1, replica_count):
            pieces.append(flipped(sent if mask % 2 else own, "dp", mask))
        normed.append(pieces)

    tensor = lax.axis_index("tensor")[None]
    own_inverse = invert_value(core, tensor, own_stats, other_stats, cotangents)
    inverses = [own_inverse, flipped(own_inverse, "dp", 1)]

    own_rows, received = [], []
    for k in range(half_blocks):
        own_rows.append(
            precondition(
                core, table, counts, normed[k], cotangents, inverses, k, half_blocks, capacity
            )
        )
        received.append(flipped(own_rows[k], "dp", 1))
    output = place_rows(core, own_rows, received)
    input_grad = finish(section, lax.axis_size("section"), top_grad, term, arrived)
    return (input_grad[None], output[None])


def solution(mesh):
    placed = (
        P("section", "dp", "tensor"),
        P("section", "tensor"),
        P("section", "tensor", None),
        P("section", "dp", None),
        P("dp", "tensor"),
        P("section", "tensor", None),
        P("section", "tensor", None),
    )
    return jax.shard_map(
        placed_work,
        mesh=mesh,
        in_specs=placed,
        out_specs=(P("section", "dp", "tensor"), P("section", "tensor", None)),
        check_vma=False,
    )
```

```python
import functools

import jax
import jax.numpy as jnp
from jax import lax
from jax.experimental import pallas as pl
from jax.experimental.pallas import tpu as pltpu
from jax.sharding import PartitionSpec as P


BLOCK = 512
EPSILON = 1e-05
DAMPING = 0.05
LANES = 128
STAT_ROWS = 8
RELAY_CHUNKS = 2
VMEM_LIMIT = 24 * 2**20


def flipped(value, axis, bit):
    count = lax.axis_size(axis)
    return lax.ppermute(value, axis, [(k, k ^ bit) for k in range(count)])


def higher_bits(axis):
    bit = 2
    while bit < lax.axis_size(axis):
        yield bit
        bit *= 2


def first_dim_product(left, right):
    return lax.dot_general(
        left, right, (((0,), (0,)), ((), ())), preferred_element_type=jnp.float32
    )


def product(left, right):
    return jnp.dot(left, right, preferred_element_type=jnp.float32)


def inverse_of(tokens, limit, state, halves):
    count, order = tokens.shape
    rows = lax.broadcasted_iota(jnp.int32, (order, order), 0)
    columns = lax.broadcasted_iota(jnp.int32, (order, order), 1)
    diagonal = rows == columns
    matrix = first_dim_product(tokens, tokens) * (1.0 / count)
    matrix = matrix + jnp.where(diagonal, DAMPING, 0.0)
    state[0] = matrix
    halves[0:order] = matrix.astype(jnp.bfloat16)
    square = product(halves[0:order], halves[0:order])
    scale = lax.rsqrt(jnp.sum(matrix * matrix))
    first = state[0] * scale
    grown = 2.0 * first - (scale * scale) * square
    start = jnp.where(diagonal, 2.0, 0.0) - first
    state[0] = start
    state[1] = grown
    halves[0:order] = start.astype(jnp.bfloat16)
    halves[order:] = grown.astype(jnp.bfloat16)

    def sweep(k, carry):
        change = product(halves[...], halves[order:])
        approx = 2.0 * state[0] - change[:order]
        grown = 2.0 * state[1] - change[order:]
        state[0] = approx
        state[1] = grown
        halves[0:order] = approx.astype(jnp.bfloat16)
        halves[order:] = grown.astype(jnp.bfloat16)
        return carry

    lax.fori_loop(2, limit, sweep, 0)
    last = 2.0 * state[0] - product(halves[0:order], halves[order:])
    return (last * scale).astype(jnp.bfloat16)


def upstream_kernel(
    table, counts, cot_hbm, weight_hbm, act_hbm, gain_hbm, scaled_ref, stats_ref, act, gain, cot, weight, sems, *, position, capacity
):
    tokens, width = act.shape
    size = BLOCK
    blocks = width // size
    small = [
        pltpu.make_async_copy(source, target, sems.at[k])
        for k, (source, target) in enumerate(((act_hbm, act), (cot_hbm, cot), (gain_hbm, gain)))
    ]
    large = [
        pltpu.make_async_copy(
            weight_hbm.at[pl.ds(k * size, size)],
            weight.at[pl.ds(k * size, size)],
            sems.at[3 + k],
        )
        for k in range(blocks)
    ]
    for copy in small + large:
        copy.start()
    small[0].wait()
    squares = jnp.zeros((tokens, LANES), jnp.float32)
    for k in range(width // LANES):
        inputs = act[:, k * LANES : (k + 1) * LANES].astype(jnp.float32)
        squares += inputs * inputs
    limit = counts[table[position] // capacity].astype(jnp.float32)
    stats_ref[...] = jnp.full(stats_ref.shape, limit, jnp.float32)
    stats_ref[0:1] = jnp.sum(squares.T, axis=0, keepdims=True)
    small[1].wait()
    small[2].wait()
    inner = jnp.zeros((tokens, LANES), jnp.float32)
    for k in range(blocks):
        span = slice(k * size, (k + 1) * size)
        large[k].wait()
        upstream = lax.dot_general(
            cot[...], weight[span], (((1,), (1,)), ((), ())), preferred_element_type=jnp.float32
        )
        scaled = upstream * gain[:, span]
        scaled_ref[:, span] = scaled
        for j in range(size // LANES):
            lanes = slice(j * LANES, (j + 1) * LANES)
            start = k * size + j * LANES
            inner += scaled[:, lanes] * act[:, start : start + LANES].astype(jnp.float32)
    stats_ref[1:2] = jnp.sum(inner.T, axis=0, keepdims=True)


SMEM = pl.BlockSpec(memory_space=pltpu.SMEM)
VMEM = pl.BlockSpec(memory_space=pltpu.VMEM)
HBM = pl.BlockSpec(memory_space=pltpu.HBM)
ANY = pl.BlockSpec(memory_space=pl.ANY)


def in_hbm(*arrays):
    return [pltpu.with_memory_space_constraint(array, pltpu.HBM) for array in arrays]


def in_vmem(*arrays):
    return [pltpu.with_memory_space_constraint(array, pltpu.VMEM) for array in arrays]


def upstream_of(table, counts, cotangent, weights, activations, gain, position, capacity):
    tokens, value_width = cotangent.shape
    width = weights.shape[0]
    return pl.pallas_call(
        functools.partial(upstream_kernel, position=position, capacity=capacity),
        in_specs=[SMEM, SMEM, HBM, HBM, HBM, HBM],
        out_specs=[VMEM] * 4,
        out_shape=[
            jax.ShapeDtypeStruct((tokens, width), jnp.float32),
            jax.ShapeDtypeStruct((STAT_ROWS, tokens), jnp.float32),
            jax.ShapeDtypeStruct(activations.shape, activations.dtype),
            jax.ShapeDtypeStruct(gain.shape, gain.dtype),
        ],
        scratch_shapes=[
            pltpu.VMEM(cotangent.shape, cotangent.dtype),
            pltpu.VMEM(weights.shape, weights.dtype),
            pltpu.SemaphoreType.DMA((3 + width // BLOCK,)),
        ],
        compiler_params=pltpu.CompilerParams(vmem_limit_bytes=VMEM_LIMIT),
        cost_estimate=pl.CostEstimate(
            flops=2 * tokens * width * value_width,
            bytes_accessed=2 * width * value_width + 8 * tokens * width,
            transcendentals=0,
        ),
        name="upstream",
    )(*in_hbm(table, counts, cotangent, weights, activations, gain))


def column(row):
    return jnp.broadcast_to(row, (LANES, row.shape[1])).T[:, :1]


def terms_kernel(core, scaled_ref, act_ref, gain_ref, own_ref, other_ref, term_ref, *refs, full_width):
    normed, chunks, pieces = refs[-1], refs[-1 - RELAY_CHUNKS : -1], refs[: -1 - RELAY_CHUNKS]
    squares = own_ref[0:1] + other_ref[0:1]
    inner_sum = own_ref[1:2] + other_ref[1:2]
    inverse_rms = lax.rsqrt(squares * (1.0 / full_width) + EPSILON)
    coefficient = inverse_rms * inverse_rms * inverse_rms * inner_sum * (1.0 / full_width)
    inverse_rms, coefficient = column(inverse_rms), column(coefficient)
    inputs = act_ref[...].astype(jnp.float32)
    normed[...] = (inputs * inverse_rms * gain_ref[...]).astype(jnp.bfloat16)
    term = inverse_rms * scaled_ref[...] - inputs * coefficient
    term_ref[...] = term.astype(jnp.bfloat16)
    for k, chunk in enumerate(chunks):
        rows = chunk.shape[0]
        chunk[...] = term[k * rows : (k + 1) * rows].astype(jnp.bfloat16)
    half = normed.shape[1] // 2
    blocks = half // BLOCK
    for k in range(blocks):
        mine = pl.multiple_of(core[0] * half + k * BLOCK, BLOCK)
        theirs = pl.multiple_of((1 - core[0]) * half + k * BLOCK, BLOCK)
        pieces[k][...] = normed[:, pl.ds(mine, BLOCK)]
        pieces[blocks + k][...] = normed[:, pl.ds(theirs, BLOCK)]


def terms_of(core, scaled, activations, gain, own_stats, other_stats, full_width):
    tokens, width = scaled.shape
    blocks = width // BLOCK
    smem = pl.BlockSpec(memory_space=pltpu.SMEM)
    vmem = pl.BlockSpec(memory_space=pltpu.VMEM)
    outs = pl.pallas_call(
        functools.partial(terms_kernel, full_width=full_width),
        in_specs=[smem] + [vmem] * 5,
        out_specs=[vmem] * (1 + blocks + RELAY_CHUNKS),
        out_shape=[jax.ShapeDtypeStruct((tokens, width), jnp.bfloat16)]
        + [jax.ShapeDtypeStruct((tokens, BLOCK), jnp.bfloat16)] * blocks
        + [jax.ShapeDtypeStruct((tokens // RELAY_CHUNKS, width), jnp.bfloat16)] * RELAY_CHUNKS,
        scratch_shapes=[pltpu.VMEM((tokens, width), jnp.bfloat16)],
        compiler_params=pltpu.CompilerParams(vmem_limit_bytes=VMEM_LIMIT),
        cost_estimate=pl.CostEstimate(
            flops=8 * tokens * width, bytes_accessed=10 * tokens * width, transcendentals=0
        ),
        name="terms",
    )(core, *in_vmem(scaled, activations, gain, own_stats, other_stats))
    split = 1 + blocks // 2
    return outs[0], outs[-RELAY_CHUNKS:], outs[1:split], outs[split:-RELAY_CHUNKS]


def payload_kernel(section, term, *refs, wave, sections):
    arrived, out = refs[:-1], refs[-1]
    rows = out.shape[0]
    chunk = jnp.minimum(jnp.maximum(wave - (sections - 1 - section[0]), 0), RELAY_CHUNKS - 1)
    total = term[pl.ds(pl.multiple_of(chunk * rows, rows), rows)].astype(jnp.float32)
    for part in arrived:
        total = total + part[...].astype(jnp.float32)
    out[...] = total.astype(jnp.bfloat16)


def payload(section, term, arrived, wave, sections):
    return pl.pallas_call(
        functools.partial(payload_kernel, wave=wave, sections=sections),
        in_specs=[SMEM] + [VMEM] * (1 + len(arrived)),
        out_specs=VMEM,
        out_shape=jax.ShapeDtypeStruct(arrived[0].shape, jnp.bfloat16),
        compiler_params=pltpu.CompilerParams(vmem_limit_bytes=VMEM_LIMIT),
        cost_estimate=pl.CostEstimate(
            flops=term.size, bytes_accessed=4 * term.size, transcendentals=0
        ),
        name="payload",
    )(section, *in_vmem(term, *arrived))


def relay(term, chunks, section, axis):
    count = lax.axis_size(axis)
    last = count - 1
    early = []
    for chunk in chunks:
        early.append(lax.ppermute(chunk, axis, [(last, last - 1)]))
    arrived = [None]
    for wave in range(1, RELAY_CHUNKS + count - 2):
        parts = [early[wave - 1]] if wave <= RELAY_CHUNKS else []
        if wave >= 2:
            parts.append(arrived[wave - 1])
        sent = payload(section, term, parts, wave, count)
        pairs = [(k, k - 1) for k in range(1, last) if 0 <= wave - (last - k) < RELAY_CHUNKS]
        arrived.append(lax.ppermute(sent, axis, pairs))
    return early, arrived[1:]


def finish_kernel(section, top_ref, term_ref, *refs, sections):
    early, arrived, out = refs[:RELAY_CHUNKS], refs[RELAY_CHUNKS:-1], refs[-1]
    rows = arrived[0].shape[0]
    for chunk in range(RELAY_CHUNKS):
        span = slice(chunk * rows, (chunk + 1) * rows)
        own = top_ref[span].astype(jnp.float32) + term_ref[span].astype(jnp.float32)

        @pl.when(section[0] == sections - 1)
        def _(span=span, own=own):
            out[span] = own.astype(jnp.bfloat16)

        for place in range(sections - 1):
            hops = sections - 2 - place
            later = arrived[chunk + hops - 1] if hops else early[chunk]

            @pl.when(section[0] == place)
            def _(span=span, own=own, later=later):
                out[span] = (own + later[...].astype(jnp.float32)).astype(jnp.bfloat16)


def finish(section, sections, top_grad, term, arrived):
    vmem = pl.BlockSpec(memory_space=pltpu.VMEM)
    return pl.pallas_call(
        functools.partial(finish_kernel, sections=sections),
        in_specs=[pl.BlockSpec(memory_space=pltpu.SMEM)] + [vmem] * (2 + len(arrived)),
        out_specs=vmem,
        out_shape=jax.ShapeDtypeStruct(term.shape, jnp.bfloat16),
        compiler_params=pltpu.CompilerParams(vmem_limit_bytes=VMEM_LIMIT),
        cost_estimate=pl.CostEstimate(
            flops=2 * term.size, bytes_accessed=8 * term.size, transcendentals=0
        ),
        name="finish",
    )(section, *in_vmem(top_grad, term, *arrived))


def scratch():
    return [
        pltpu.VMEM((2, BLOCK, BLOCK), jnp.float32),
        pltpu.VMEM((2 * BLOCK, BLOCK), jnp.bfloat16),
    ]


def value_kernel(core, tensor, own_stats, other_stats, *refs, pieces):
    span = pl.ds(pl.multiple_of(core[0] * BLOCK, BLOCK), BLOCK)
    tokens = jnp.concatenate([ref[:, span] for ref in refs[:pieces]], axis=0)
    out, state, halves = refs[pieces:]
    own_limit, other_limit = jnp.max(own_stats[2:3]), jnp.max(other_stats[2:3])
    limit = jnp.where(core[0] == tensor[0], own_limit, other_limit).astype(jnp.int32)
    out[...] = inverse_of(tokens, limit, state, halves)


def invert_value(core, tensor, own_stats, other_stats, pieces):
    return pl.pallas_call(
        functools.partial(value_kernel, pieces=len(pieces)),
        in_specs=[SMEM, SMEM] + [VMEM] * (2 + len(pieces)),
        out_specs=VMEM,
        scratch_shapes=scratch(),
        out_shape=jax.ShapeDtypeStruct((BLOCK, BLOCK), jnp.bfloat16),
        compiler_params=pltpu.CompilerParams(vmem_limit_bytes=VMEM_LIMIT),
        cost_estimate=pl.CostEstimate(
            flops=22 * BLOCK**3, bytes_accessed=4 * BLOCK**2, transcendentals=0
        ),
        name="value_inverse",
    )(core, tensor, *in_vmem(own_stats, other_stats, *pieces))


def feature_kernel(core, table, counts, *refs, pieces, place, half_blocks, capacity):
    normed = jnp.concatenate([ref[...] for ref in refs[:pieces]], axis=0)
    own_inverse, other_inverse = refs[2 * pieces], refs[2 * pieces + 1]
    out, state, halves, left = refs[-4:]
    owner = table[core[0] * half_blocks + place] // capacity
    inverse = inverse_of(normed, counts[owner], state, halves)
    cotangent = jnp.concatenate([ref[...] for ref in refs[pieces : 2 * pieces]], axis=0)
    grad = first_dim_product(normed, cotangent).astype(jnp.bfloat16)
    left[...] = product(inverse, grad).astype(jnp.bfloat16)
    for turn, value_inverse in ((0, own_inverse), (1, other_inverse)):
        block = core[0] if turn == 0 else 1 - core[0]
        span = pl.ds(pl.multiple_of(block * BLOCK, BLOCK), BLOCK)
        out[:, span] = product(left[:, span], value_inverse[...]).astype(jnp.bfloat16)


def precondition(core, table, counts, normed, cotangents, inverses, place, half_blocks, capacity):
    value_width = cotangents[0].shape[1]
    pieces = len(normed)
    return pl.pallas_call(
        functools.partial(
            feature_kernel, pieces=pieces, place=place, half_blocks=half_blocks, capacity=capacity
        ),
        in_specs=[SMEM] * 3 + [VMEM] * (2 * pieces + 2),
        out_specs=VMEM,
        scratch_shapes=scratch() + [pltpu.VMEM((BLOCK, value_width), jnp.bfloat16)],
        out_shape=jax.ShapeDtypeStruct((BLOCK, value_width), jnp.bfloat16),
        compiler_params=pltpu.CompilerParams(vmem_limit_bytes=VMEM_LIMIT),
        cost_estimate=pl.CostEstimate(
            flops=34 * BLOCK**3, bytes_accessed=8 * BLOCK**2, transcendentals=0
        ),
        name="precondition",
    )(core, *in_hbm(table, counts), *in_vmem(*normed, *cotangents, *inverses))


def place_kernel(core, *refs, blocks):
    pieces, out, sems = refs[: 2 * blocks], refs[-2], refs[-1]
    copies = []
    for k, piece in enumerate(pieces):
        owner = core[0] if k < blocks else 1 - core[0]
        start = pl.multiple_of((owner * blocks + k % blocks) * BLOCK, BLOCK)
        copies.append(pltpu.make_async_copy(piece, out.at[pl.ds(start, BLOCK)], sems.at[k]))
    for copy in copies:
        copy.start()
    for copy in copies:
        copy.wait()


def place_rows(core, own, received):
    blocks = len(received)
    value_width = received[0].shape[1]
    return pl.pallas_call(
        functools.partial(place_kernel, blocks=blocks),
        in_specs=[SMEM] + [VMEM] * (2 * blocks),
        out_specs=HBM,
        out_shape=jax.ShapeDtypeStruct((2 * blocks * BLOCK, value_width), jnp.bfloat16),
        scratch_shapes=[pltpu.SemaphoreType.DMA((2 * blocks,))],
        compiler_params=pltpu.CompilerParams(vmem_limit_bytes=VMEM_LIMIT),
        cost_estimate=pl.CostEstimate(
            flops=0, bytes_accessed=8 * blocks * BLOCK * value_width, transcendentals=0
        ),
        name="place_rows",
    )(core, *in_vmem(*own, *received))


def placed_work(activations, norm_gain, weights, cotangent, top_grad, owner_slot, sweeps):
    acts, cot = activations[0], cotangent[0]
    table, counts = owner_slot[0, 0], sweeps[0, 0]
    _, half_width = acts.shape
    value_width = cot.shape[1]
    tensor_size = lax.axis_size("tensor")
    replica_count = lax.axis_size("dp")
    feature_blocks = half_width // BLOCK
    value_blocks = value_width // BLOCK
    unit_count = feature_blocks + 1 + feature_blocks * value_blocks
    capacity = (unit_count + replica_count - 1) // replica_count
    half_blocks = feature_blocks // 2
    core = (lax.axis_index("dp") % 2)[None]

    far = [cot]
    for bit in higher_bits("dp"):
        far = far + [flipped(piece, "dp", bit) for piece in far]
    cotangents = []
    for piece in far:
        cotangents += [piece, flipped(piece, "dp", 1)]

    scaled, own_stats, local_acts, local_gain = upstream_of(
        table, counts, cot, weights[0], acts, norm_gain, feature_blocks, capacity
    )
    other_stats = flipped(own_stats, "tensor", 1)
    term, chunks, mine, theirs = terms_of(
        core, scaled, local_acts, local_gain, own_stats, other_stats, half_width * tensor_size
    )
    section = lax.axis_index("section")[None]
    early, arrived = relay(term, chunks, section, "section")

    normed = []
    for own, sent in zip(mine, theirs):
        pieces = [own]
        for mask in range(1, replica_count):
            pieces.append(flipped(sent if mask % 2 else own, "dp", mask))
        normed.append(pieces)

    tensor = lax.axis_index("tensor")[None]
    own_inverse = invert_value(core, tensor, own_stats, other_stats, cotangents)
    inverses = [own_inverse, flipped(own_inverse, "dp", 1)]

    own_rows, received = [], []
    for k in range(half_blocks):
        own_rows.append(
            precondition(
                core, table, counts, normed[k], cotangents, inverses, k, half_blocks, capacity
            )
        )
        received.append(flipped(own_rows[k], "dp", 1))
    output = place_rows(core, own_rows, received)
    input_grad = finish(section, lax.axis_size("section"), top_grad, term, early + arrived)
    return (input_grad[None], output[None])


def solution(mesh):
    placed = (
        P("section", "dp", "tensor"),
        P("section", "tensor"),
        P("section", "tensor", None),
        P("section", "dp", None),
        P("dp", "tensor"),
        P("section", "tensor", None),
        P("section", "tensor", None),
    )
    return jax.shard_map(
        placed_work,
        mesh=mesh,
        in_specs=placed,
        out_specs=(P("section", "dp", "tensor"), P("section", "tensor", None)),
        check_vma=False,
    )
```
